256 devices in a mesh: ckpt: 16 (over y_hi, x, core), lat: 16 (over y_lo, z).
Axes of the slice: x: 4, y: 4 (y_hi: 2, y_lo: 2; y = y_hi * 2 + y_lo), z: 8, core: 2. Of those that a mesh axis runs over, the one named last changes fastest.
Arguments:
- hidden_in: bfloat16 [32, 512, 1024], P('ckpt', None, 'lat'), may hold values from -6 to 6
- ln_gain: float32 [32, 1024], P('ckpt'), may hold values from 0.4 to 1.6
- ln_bias: float32 [32, 1024], P('ckpt'), may hold values from -2.5 to 2.5
- w_in: bfloat16 [32, 1024, 4096], P('ckpt', None, 'lat'), may hold values from -0.1875 to 0.1875
- b_in: float32 [32, 4096], P('ckpt', 'lat'), may hold values from -3 to 3
- w_out: bfloat16 [32, 4096, 1024], P('ckpt', 'lat'), may hold values from -0.09375 to 0.09375
- b_out: float32 [32, 1024], P('ckpt'), may hold values from -3 to 3
- w_enc: bfloat16 [32, 1024, 8192], P('ckpt', None, 'lat'), may hold values from -0.03125 to 0.03125
- b_enc: float32 [8192], P('lat'), may hold values from -3 to 3
- w_dec: bfloat16 [32, 8192, 1024], P('ckpt', 'lat'), may hold values from -6 to 6
- b_dec: float32 [32, 1024], P('ckpt'), may hold values from -3 to 3
Outputs:
- grad_enc: bfloat16 [32, 1024, 8192], P('ckpt', None, 'lat')
- grad_benc: float32 [8192], P('lat')
- grad_dec: bfloat16 [32, 8192, 1024], P('ckpt', 'lat')
The draws below stay inside these ranges and needn't reach their ends.
All inputs are finite; a program needn't handle non-finite values.
Results may differ from the reference program's by a relative error of at most 0.0075.
Values may be sent and summed in bfloat16 or wider, within the bound.
No kernel may reach another device: no remote copies, remote signals or barrier semaphores. Data moves between devices by JAX's collectives and lax.ppermute only.
A program may use at most 64 MiB of HBM per device.

```python
import math
import jax
import jax.numpy as jnp
from jax import lax

D = 1024
FF = 4096
LATENTS = 8192
TOK = 512
CKPTS = 32


def draw_w_dec(key, part):
    base = jax.random.normal(jax.random.fold_in(key, 11), (CKPTS, LATENTS, D), jnp.float32)
    base = jnp.clip(base, -6.0, 6.0) / jnp.sqrt(jnp.float32(LATENTS))
    place = jnp.arange(CKPTS).astype(jnp.float32) / jnp.float32(max(CKPTS - 1, 1)) - 0.5
    ramp = jnp.exp(jnp.log(6.0) * place)
    return jnp.clip(base * ramp[:, None, None], -6.0, 6.0).astype(jnp.bfloat16)


def block_scale(stream_key, dims, shards, least, top_value):
    def one(dim, shards_of):
        draws = jax.random.uniform(jax.random.fold_in(jax.random.fold_in(stream_key, 6), dim), (shards_of,), jnp.float32, least / len(shards), top_value / len(shards))
        return jnp.repeat(jnp.exp(draws), dims[dim] // shards_of).reshape((-1,) + (1,) * (len(dims) - dim - 1))

    loudness = one(*shards[0])
    for cut in shards[1:]:
        loudness = loudness * one(*cut)
    return loudness


def centred(own_key, extent, scale, limit, cuts=(), kind=jnp.bfloat16):
    drawn = scale * jax.random.normal(own_key, extent, jnp.float32)
    if cuts:
        drawn = drawn * block_scale(own_key, extent, cuts, -0.22, 0.18)
    return jnp.clip(drawn, -limit, limit).astype(kind)


def setup_inputs(seed: int = 0) -> dict:
    keys = jax.random.split(jax.random.key(seed), 12)
    return {
        "hidden_in": centred(keys[0], (CKPTS, TOK, D), 1.0, 6.0, ((0, 16), (2, 16))),
        "ln_gain": jnp.clip(1.0 + 0.12 * jax.random.normal(keys[1], (CKPTS, D), jnp.float32), 0.4, 1.6),
        "ln_bias": centred(keys[2], (CKPTS, D), 0.4, 2.5, ((0, 16),), jnp.float32),
        "w_in": centred(keys[3], (CKPTS, D, FF), D ** -0.5, 0.1875, ((0, 16), (2, 16))),
        "b_in": centred(keys[4], (CKPTS, FF), 0.5, 3.0, ((0, 16), (1, 16)), jnp.float32),
        "w_out": centred(keys[5], (CKPTS, FF, D), FF ** -0.5, 0.09375, ((0, 16), (1, 16))),
        "b_out": centred(keys[6], (CKPTS, D), 0.5, 3.0, ((0, 16),), jnp.float32),
        "w_enc": centred(keys[7], (CKPTS, D, LATENTS), (CKPTS * D) ** -0.5, 0.03125, ((0, 16), (2, 16))),
        "b_enc": centred(keys[8], (LATENTS,), 0.5, 3.0, ((0, 16),), jnp.float32),
        "w_dec": draw_w_dec(jax.random.fold_in(keys[11], 71), 0),
        "b_dec": centred(keys[10], (CKPTS, D), 0.5, 3.0, ((0, 16),), jnp.float32),
    }


norm_eps = 1e-05
row_eps = 1e-06
sparsity_weight = 0.2

def section_one(parts):
    hidden, gain, bias, w_first, b_first, w_second, b_second = parts
    floats = hidden.astype(jnp.float32)
    center = floats - lax.optimization_barrier(jnp.mean(floats, -1, keepdims=True))
    spread = lax.optimization_barrier(jnp.mean(center * center, -1, keepdims=True))
    normed = (center * lax.rsqrt(spread + norm_eps) * gain + bias).astype(jnp.bfloat16)
    raised = jnp.dot(normed, w_first, preferred_element_type=jnp.float32) + b_first
    active = jax.nn.gelu(raised, approximate=False).astype(jnp.bfloat16)
    return (floats + jnp.dot(active, w_second, preferred_element_type=jnp.float32) + b_second).astype(jnp.bfloat16)

def reference(hidden_in, ln_gain, ln_bias, w_in, b_in, w_out, b_out, w_enc, b_enc, w_dec, b_dec):
    scale = 1.0 / math.sqrt(TOK)
    acts = lax.map(section_one, (hidden_in, ln_gain, ln_bias, w_in, b_in, w_out, b_out))

    def add_encoded(carry, pair):
        return (carry + jnp.dot(pair[0], pair[1], preferred_element_type=jnp.float32), None)
    pre = lax.scan(add_encoded, jnp.zeros((TOK, LATENTS), jnp.float32), (acts, w_enc))[0] + b_enc
    feat = jnp.maximum(pre, 0.0).astype(jnp.bfloat16)

    def row_norms(weight):
        wide = weight.astype(jnp.float32)
        return jnp.sqrt(lax.optimization_barrier(jnp.sum(wide * wide, -1)) + row_eps)
    norms = lax.map(row_norms, w_dec)
    total = lax.optimization_barrier(jnp.sum(norms, 0))

    def residual(parts):
        act, weight, bias = parts
        resid = jnp.dot(feat, weight, preferred_element_type=jnp.float32) + bias - act.astype(jnp.float32)
        return (resid * scale).astype(jnp.bfloat16)
    dres = lax.map(residual, (acts, w_dec, b_dec))

    def add_back(carry, pair):
        return (carry + jnp.dot(pair[0], pair[1].T, preferred_element_type=jnp.float32), None)
    dfeat = lax.scan(add_back, jnp.zeros((TOK, LATENTS), jnp.float32), (dres, w_dec))[0]
    dfeat = dfeat + sparsity_weight * scale * total
    dpre = jnp.where(pre > 0.0, dfeat, 0.0).astype(jnp.bfloat16)

    def encoder_grad(act):
        return jnp.dot(act.T, dpre, preferred_element_type=jnp.float32).astype(jnp.bfloat16)
    grad_enc = lax.map(encoder_grad, acts)
    grad_benc = lax.optimization_barrier(jnp.sum(dpre.astype(jnp.float32), 0))
    column = lax.optimization_barrier(jnp.sum(feat.astype(jnp.float32), 0))

    def decoder_grad(parts):
        grads, weight, norm_row = parts
        main = jnp.dot(feat.T, grads, preferred_element_type=jnp.float32)
        extra = sparsity_weight * scale * column[:, None] * weight.astype(jnp.float32) / norm_row[:, None]
        return (main + extra).astype(jnp.bfloat16)
    grad_dec = lax.map(decoder_grad, (dres, w_dec, norms))
    return (grad_enc, grad_benc, grad_dec)
```

```python
import math

import jax
import jax.numpy as jnp
from jax import lax
from jax.sharding import Mesh
from jax.sharding import PartitionSpec as P

CKPT = ("yh", "x", "core")
LAT = ("yl", "z")
XY = ("yh", "yl", "x")
PLANE = 16

norm_eps = 1e-05
row_eps = 1e-06
sparsity_weight = 0.2


def shift(value, axis, by):
    n = lax.axis_size(axis)
    return lax.ppermute(value, axis, [(i, (i + by) % n) for i in range(n)])


def take(blocks, i, dim=0):
    return lax.dynamic_index_in_dim(blocks, i, dim, keepdims=False)


def put(out, value, i, dim):
    return lax.dynamic_update_index_in_dim(out, value, i, dim)


def after(value, *others):
    return lax.optimization_barrier((value, *others))[0]


def pair_in_order(mine, got, first):
    return jnp.where(first, jnp.stack([mine, got]), jnp.stack([got, mine]))


def ring_sum(blocks, axis, dim):
    n = lax.axis_size(axis)
    me = lax.axis_index(axis)
    wire = blocks.dtype
    half = n // 2
    again = after(blocks)

    def block(k):
        source = blocks if k >= 0 else again
        return take(source, lax.rem(me + k + n, n), dim).astype(jnp.float32)

    def send(value, by):
        return shift(value.astype(wire), axis, by).astype(jnp.float32)

    up = send(block(half), 1)
    down = send(block(1 - half), -1)
    for step in range(2, half + 1):
        up = block(half + 1 - step) + up
        up = send(up, 1)
        if step < half:
            down = block(step - half) + down
            down = send(down, -1)
    return block(0) + up + down


def ring_all(mine, axis, dim, relay=None):
    n = lax.axis_size(axis)
    me = lax.axis_index(axis)
    half = n // 2

    def at(k):
        return lax.rem(me + k + n, n)

    def empty():
        return jnp.broadcast_to(
            jnp.expand_dims(mine, dim), (*mine.shape[:dim], n, *mine.shape[dim:])
        )

    def pass_on(last, *parts):
        if relay:
            value = shift(jnp.stack(parts), "yl", 1)
            theirs.append((last, value))

    theirs = []
    out = empty()
    up = down = mine
    for k in range(1, half):
        up, down = shift(up, axis, 1), shift(down, axis, -1)
        if k == 1:
            pass_on(k, up, down, mine)
        elif k < half - 1:
            pass_on(k, up, down)
        out = put(out, up, at(-k), dim)
        out = put(out, down, at(k), dim)
    far = shift(up, axis, 1)
    pass_on(half - 1, up, down, far)
    out = put(out, far, at(half), dim)
    if not relay:
        return out
    other = empty()
    for k, value in theirs:
        other = put(other, value[0], at(-k), dim)
        other = put(other, value[1], at(k), dim)
        if len(value) > 2:
            other = put(other, value[2], at(0 if k == 1 else half), dim)
    return out, other


def exchange(blocks, axis):
    return lax.all_to_all(blocks, axis, 0, 0, tiled=True)


def everyone(block, axis):
    n = lax.axis_size(axis)
    return exchange(jnp.broadcast_to(block[None], (n, *block.shape)), axis)


def core_sum(blocks, core):
    give = take(blocks, 1 - core, 1)
    return take(blocks, core, 1).astype(jnp.float32) + shift(give, "core", 1).astype(jnp.float32)


def core_all(mine, core, dim):
    out = jnp.zeros((*mine.shape[:dim], 2, *mine.shape[dim:]), mine.dtype)
    out = put(out, mine, core, dim)
    return put(out, shift(mine, "core", 1), 1 - core, dim)


def plane_sum(partial, side):
    core = lax.axis_index("core")
    wire = partial.dtype
    lat, tok = partial.shape[1:]
    halves = partial.reshape(2, 2, lat // 2, tok)
    part = core_sum(halves, core).astype(wire).reshape(2, PLANE, lat // 2 // PLANE, tok)
    part = jnp.stack([take(part, side), take(part, 1 - side)], 1)
    arrived = exchange(part, XY)
    total = jnp.sum(arrived.astype(jnp.float32), 0)
    return jnp.stack([take(total, side), take(total, 1 - side)])


def plane_all(share, side):
    core = lax.axis_index("core")
    rows, tok = share.shape[1:]
    share = jnp.stack([take(share, side), take(share, 1 - side)])
    out = everyone(share, XY)
    out = jnp.stack([take(out, side, 1), take(out, 1 - side, 1)])
    out = core_all(out.reshape(2, PLANE * rows, tok), core, 1)
    return out.reshape(2, 2 * PLANE * rows, tok)


def plane_all_own(share, side):
    core = lax.axis_index("core")
    rows, tok = share.shape[1:]
    share = jnp.stack([take(share, side), take(share, 1 - side)])
    share = jnp.broadcast_to(share[None, :, None], (2, 2, 4, rows, tok)).reshape(PLANE, rows, tok)
    out = exchange(share, XY)
    out = core_all(out.reshape(PLANE * rows, tok), core, 0)
    return out.reshape(2 * PLANE * rows, tok)


def on_device(hidden_in, ln_gain, ln_bias, w_in, b_in, w_out, b_out, w_enc, b_enc, w_dec, b_dec):
    tokens = hidden_in.shape[1]
    cols = hidden_in.shape[2]
    width = ln_gain.shape[1]
    lats = w_dec.shape[1]
    scale = 1.0 / math.sqrt(tokens)
    side = lax.axis_index("yl")
    z = lax.axis_index("z")
    zs = lax.axis_size("z")
    first = side == 0

    def mine(v):
        return take(v, side)

    def swapped(v, *order):
        return shift(take(after(v, *order) if order else v, 1 - side), "yl", 1)

    def own_rows(v):
        return take(mine(v).reshape(2, zs, cols), z, 1)[:, :, None]

    turned = hidden_in.transpose(0, 2, 1)
    got_hidden = swapped(turned)
    hidden = pair_in_order(mine(turned), got_hidden, first)
    whole = ring_all(hidden, "z", 1).reshape(width, tokens)
    got = [swapped(v, got_hidden) for v in (w_in, b_in, w_out)]
    *got, whole = lax.optimization_barrier((*got, whole))
    first_w = jnp.concatenate([mine(w_in), got[0]], 1)
    first_b = jnp.concatenate([mine(b_in), got[1]], 0)
    second_w = jnp.concatenate([mine(w_out), got[2]], 0)

    floats = whole.astype(jnp.float32)
    center = floats - jnp.mean(floats, 0, keepdims=True)
    spread = jnp.mean(center * center, 0, keepdims=True)
    normed = (
        center * lax.rsqrt(spread + norm_eps) * mine(ln_gain)[:, None] + mine(ln_bias)[:, None]
    ).astype(jnp.bfloat16)
    raised = (
        jnp.einsum("df,dt->ft", first_w, normed, preferred_element_type=jnp.float32)
        + first_b[:, None]
    )
    active = jax.nn.gelu(raised, approximate=False).astype(jnp.bfloat16)
    terms = jnp.einsum("fd,ft->dt", second_w, active, preferred_element_type=jnp.float32)
    got_enc = swapped(w_enc, whole)
    share = ring_sum(terms.reshape(2, zs, cols, tokens), "z", 1)
    piece = (hidden.astype(jnp.float32) + share + own_rows(b_out)).astype(jnp.bfloat16)
    acts = ring_all(piece, "z", 1).reshape(width, tokens)
    enc = jnp.concatenate([mine(w_enc), after(got_enc, acts)], 1)
    got_dec = swapped(w_dec, whole)

    adds_bias = lax.axis_index(CKPT) == 0
    bias = jnp.concatenate([jnp.where(adds_bias, b_enc, 0.0), jnp.zeros_like(b_enc)])
    pre_terms = (
        jnp.einsum("dl,dt->lt", enc, acts, preferred_element_type=jnp.float32) + bias[:, None]
    )
    pre = plane_sum(pre_terms.reshape(2, lats, tokens), side)
    feat = plane_all(jnp.maximum(pre, 0.0).astype(jnp.bfloat16), side)

    dec = jnp.concatenate([mine(w_dec), after(got_dec, pre)], 0)
    recon = jnp.einsum(
        "ld,lt->dt", dec, feat.reshape(2 * lats, tokens), preferred_element_type=jnp.float32
    ).astype(jnp.bfloat16)
    got_acts = shift(after(acts, recon), "yl", 1)
    recon_share = ring_sum(recon.reshape(2, zs, cols, tokens), "z", 1)
    resid = recon_share + own_rows(b_dec) - piece.astype(jnp.float32)
    dres, other_dres = ring_all((resid * scale).astype(jnp.bfloat16), "z", 1, "y_dres")
    dres = dres.reshape(width, tokens)
    other_dres = other_dres.reshape(width, tokens)
    all_acts = pair_in_order(acts, after(got_acts, dres), first)

    wide = dec.astype(jnp.float32)
    line_norms = jnp.sqrt(jnp.sum(wide * wide, 1) + row_eps)
    back = jnp.einsum("ld,dt->lt", dec, dres, preferred_element_type=jnp.float32)
    dfeat_terms = (
        back
        + (sparsity_weight * scale) * line_norms[:, None]
    ).astype(jnp.bfloat16)
    dfeat = plane_sum(dfeat_terms.reshape(2, lats, tokens), side)
    all_dres = pair_in_order(dres, other_dres, first)
    dpre = plane_all_own(jnp.where(pre > 0.0, dfeat, 0.0).astype(jnp.bfloat16), side)

    grad_enc = jnp.einsum("cdt,lt->cdl", all_acts, dpre, preferred_element_type=jnp.float32).astype(
        jnp.bfloat16
    )
    grad_benc = jnp.sum(dpre.astype(jnp.float32), 1)
    own_feat = feat[0]
    wide_dec = w_dec.astype(jnp.float32)
    norms = jnp.sqrt(jnp.sum(wide_dec * wide_dec, 2) + row_eps)
    column = jnp.sum(own_feat.astype(jnp.float32), 1)
    twice = jnp.broadcast_to(own_feat[None], (2, *own_feat.shape))
    main = jnp.einsum("clt,cdt->cld", twice, all_dres, preferred_element_type=jnp.float32)
    extra = sparsity_weight * scale * column[None, :, None] * wide_dec / norms[:, :, None]
    grad_dec = (main + extra).astype(jnp.bfloat16)
    return (grad_enc, grad_benc, grad_dec)


def solution(mesh):
    torus = Mesh(mesh.devices.reshape(2, 4, 2, 2, 8), ("yh", "x", "core", "yl", "z"))
    placed = (
        P(CKPT, None, LAT),
        P(CKPT, None),
        P(CKPT, None),
        P(CKPT, None, LAT),
        P(CKPT, LAT),
        P(CKPT, LAT, None),
        P(CKPT, None),
        P(CKPT, None, LAT),
        P(LAT),
        P(CKPT, LAT, None),
        P(CKPT, None),
    )
    return jax.shard_map(
        on_device,
        mesh=torus,
        in_specs=placed,
        out_specs=(P(CKPT, None, LAT), P(LAT), P(CKPT, LAT, None)),
        check_vma=False,
    )
```
